256 devices in a mesh: frame: 16 (over z_hi, y, core), row: 16 (over x, z_lo).
Axes of the slice: x: 4, y: 4, z: 8 (z_hi: 2, z_lo: 4; z = z_hi * 4 + z_lo), core: 2. Of those that a mesh axis runs over, the one named last changes fastest.
Arguments:
- features: float32 [16, 64, 256, 256], P('frame', 'row'), may hold values from -6 to 6
- conv_weight: float32 [2, 3, 3, 256, 256], replicated, may hold values from -0.125 to 0.125
Outputs:
- activations: float32 [16, 64, 256, 256], P('frame', 'row')
The draws below stay inside these ranges and needn't reach their ends.
All inputs are finite; a program needn't handle non-finite values.
Results may differ from the reference program's by a relative error of at most 0.0001.
Values sent between devices are 32-bit elements; how exact they have to be, the bound alone decides.
No kernel may reach another device: no remote copies, remote signals or barrier semaphores. Data moves between devices by JAX's collectives and lax.ppermute only.
A program may use at most 64 MiB of HBM per device.

```python
import jax
import jax.numpy as jnp
from jax import lax

C = 256
W = 256
LAYERS = 2
FRAMES = 16
H = 64


def block_levels(key, shape, shards, least, top_value):
    def one(position, shards_of):
        steps = jax.random.uniform(jax.random.fold_in(jax.random.fold_in(key, 6), position), (shards_of,), jnp.float32, least / len(shards), top_value / len(shards))
        return jnp.repeat(jnp.exp(steps), shape[position] // shards_of).reshape((-1,) + (1,) * (len(shape) - position - 1))

    factor_of = one(*shards[0])
    for cut in shards[1:]:
        factor_of = factor_of * one(*cut)
    return factor_of


def scatter_about(key, dims, deviation, reach, pieces=(), kind=jnp.bfloat16):
    factor_of = block_levels(key, dims, pieces, -0.22, 0.18) if pieces else 1.0
    result = jax.random.normal(key, dims, jnp.float32) * deviation * factor_of
    return jnp.minimum(jnp.maximum(result, -reach), reach).astype(kind)


def setup_inputs(seed: int = 0) -> dict:
    keys = jax.random.split(jax.random.key(seed), 3)
    features = scatter_about(keys[0], (FRAMES, H, W, C), 1.0, 6.0, ((0, 16), (1, 16)), jnp.float32)
    conv_weight = scatter_about(keys[1], (LAYERS, 3, 3, C, C), (9 * C) ** -0.5, 0.125, (), jnp.float32)
    return dict(features=features, conv_weight=conv_weight)


def temporal_shift(field):
    fold = field.shape[3] // 8
    zeros = jnp.zeros_like(field[:1, :, :, :fold])
    from_next = jnp.concatenate([field[1:, :, :, :fold], zeros], axis=0)
    from_prev = jnp.concatenate([zeros, field[:-1, :, :, fold:2 * fold]], axis=0)
    return jnp.concatenate([from_next, from_prev, field[:, :, :, 2 * fold:]], axis=3)


def convolve_frame(frame, kernel):
    rows, cols, chans = frame.shape
    padded = jnp.pad(frame, ((1, 1), (1, 1), (0, 0)))
    total = jnp.zeros((rows * cols, kernel.shape[3]), jnp.float32)
    for tap_row in range(3):
        for tap_col in range(3):
            window = padded[tap_row:tap_row + rows, tap_col:tap_col + cols, :].reshape(rows * cols, chans)
            total = total + jnp.dot(window, kernel[tap_row, tap_col], preferred_element_type=jnp.float32, precision=lax.Precision.HIGHEST)
    return jnp.maximum(total, 0.0).reshape(rows, cols, kernel.shape[3])


def reference(features, conv_weight):
    field = features
    for layer in range(LAYERS):
        shifted = temporal_shift(field)
        kernel = conv_weight[layer]
        field = lax.map(lambda frame: convolve_frame(frame, kernel), shifted)
    return field
```

```python
import jax
import jax.numpy as jnp
from jax import lax
from jax.experimental import pallas as pl
from jax.experimental.pallas import tpu as pltpu
from jax.sharding import PartitionSpec as P

F32 = jnp.float32
BF16 = jnp.bfloat16
VMEM = pl.BlockSpec(memory_space=pltpu.VMEM)
PARAMS = pltpu.CompilerParams(vmem_limit_bytes=48 * 2**20)


def exchange(block, axis, odd):
    count = lax.axis_size(axis)
    pairs = [(i, i + 1) for i in range(odd, count - 1, 2)]
    return lax.ppermute(block, axis, pairs + [(b, a) for a, b in pairs])


def parts(x):
    hi = x.astype(BF16)
    return hi, (x - hi.astype(F32)).astype(BF16)


def dot(a, b):
    return jnp.dot(a, b, preferred_element_type=F32)


def dot3(ah, al, bh, bl):
    return dot(ah, bh) + (dot(al, bh) + dot(ah, bl))


def join_columns(left, mid, right):
    cols = mid.shape[0]
    at = lax.broadcasted_iota(jnp.int32, mid.shape, 0)
    left = jnp.where(at == 0, 0.0, pltpu.roll(left, 1, 0))
    right = jnp.where(at == cols - 1, 0.0, pltpu.roll(right, cols - 1, 0))
    return mid + left + right


def pack(row, first, fold):
    blocks = 128 // fold
    height = row.shape[0] // blocks
    lane = lax.broadcasted_iota(jnp.int32, (height, 128), 1) // fold
    out = jnp.zeros((height, 128), F32)
    for j in range(blocks):
        piece = pltpu.roll(row[j * height : (j + 1) * height, :128], (j * fold - first) % 128, 1)
        out = jnp.where(lane == j, piece, out)
    return out


def shifted_lanes(lanes, following, before, fold):
    blocks = 128 // fold
    height = following.shape[0]
    lane = lax.broadcasted_iota(jnp.int32, (height, 128), 1)
    pieces = []
    for j in range(blocks):
        nxt = pltpu.roll(following, (-j * fold) % 128, 1)
        prv = pltpu.roll(before, (fold - j * fold) % 128, 1)
        own = lanes[j * height : (j + 1) * height]
        pieces.append(jnp.where(lane < fold, nxt, jnp.where(lane < 2 * fold, prv, own)))
    return jnp.concatenate(pieces, axis=0)


def split_weights_kernel(w_ref, hi_ref, lo_ref):
    hi, lo = parts(w_ref[...])
    hi_ref[...] = hi
    lo_ref[...] = lo


def split_weights(weight):
    spec = pl.BlockSpec((1, 1) + weight.shape[2:], lambda l, i: (l, i, 0, 0, 0))
    return pl.pallas_call(
        split_weights_kernel,
        grid=weight.shape[:2],
        in_specs=[spec],
        out_specs=[spec, spec],
        out_shape=[jax.ShapeDtypeStruct(weight.shape, BF16)] * 2,
        name="split_weights",
    )(weight)


def by_parity(axis, even_case, odd_case):
    parity = lax.axis_index(axis) % 2
    pl.when(parity == 0)(even_case)
    pl.when(parity == 1)(odd_case)


def pack_kernel(x_ref, even_ref, odd_ref):
    fold = even_ref.shape[1] * 128 // x_ref.shape[1]

    def write(to_before, to_following):
        for r in range(x_ref.shape[0]):
            row = x_ref[r]
            to_before[r] = pack(row, 0, fold)
            to_following[r] = pack(row, fold, fold)

    by_parity("frame", lambda: write(odd_ref, even_ref), lambda: write(even_ref, odd_ref))


def pack_frames(x, fold):
    rows, cols, chans = x.shape
    packed = jax.ShapeDtypeStruct((rows, cols * fold // 128, 128), F32)
    return pl.pallas_call(
        pack_kernel,
        grid=(1,),
        in_specs=[pl.BlockSpec((rows, cols, 128), lambda i: (0, 0, 0))],
        out_specs=[pl.BlockSpec(packed.shape, lambda i: (0, 0, 0))] * 2,
        out_shape=[packed, packed],
        name="pack_frames",
        compiler_params=PARAMS,
    )(x)


def edge_rows_kernel(x_ref, feven_ref, fodd_ref, reven_ref, rodd_ref):
    rows, cols, chans = x_ref.shape
    fold = feven_ref.shape[1] * 128 // cols

    def write(following, before, first_to, last_to):
        for r, out in ((0, first_to), (rows - 1, last_to)):
            out[:, :128] = shifted_lanes(x_ref[r, :, :128], following[r], before[r], fold)
            out[:, 128:] = x_ref[r, :, 128:]

    def rows_case(first_to, last_to):
        by_parity(
            "frame",
            lambda: write(feven_ref, fodd_ref, first_to, last_to),
            lambda: write(fodd_ref, feven_ref, first_to, last_to),
        )

    by_parity("row", lambda: rows_case(rodd_ref, reven_ref), lambda: rows_case(reven_ref, rodd_ref))


def edge_rows(x, feven, fodd):
    rows, cols, chans = x.shape
    edge = jax.ShapeDtypeStruct((cols, chans), F32)
    return pl.pallas_call(
        edge_rows_kernel,
        in_specs=[VMEM] * 3,
        out_specs=[VMEM] * 2,
        out_shape=[edge, edge],
        name="edge_rows",
        compiler_params=PARAMS,
    )(x, feven, fodd)


def inner_kernel(x_ref, feven_ref, fodd_ref, wh_ref, wl_ref, out_ref, hi, lo, acc):
    rows, cols, chans = x_ref.shape
    fold = feven_ref.shape[1] * 128 // cols

    def write(following, before):
        for r in range(rows):
            lanes = shifted_lanes(x_ref[r, :, :128], following[r], before[r], fold)
            at = slice(r * cols, (r + 1) * cols)
            hi[at, :128], lo[at, :128] = parts(lanes)
            hi[at, 128:], lo[at, 128:] = parts(x_ref[r, :, 128:])

    by_parity("frame", lambda: write(feven_ref, fodd_ref), lambda: write(fodd_ref, feven_ref))
    for dx in range(3):
        for dy in (1, 0, 2):
            source = slice(max(dy - 1, 0) * cols, (rows + min(dy - 1, 0)) * cols)
            target = slice(max(1 - dy, 0) * cols, (rows + min(1 - dy, 0)) * cols)
            part = dot3(hi[source], lo[source], wh_ref[dy, dx], wl_ref[dy, dx])
            if dy == 1:
                acc[dx] = part
            else:
                acc[dx, target] += part
    for r in range(rows):
        at = slice(r * cols, (r + 1) * cols)
        total = join_columns(acc[0, at], acc[1, at], acc[2, at])
        out_ref[r] = total if r in (0, rows - 1) else jnp.maximum(total, 0.0)


def inner_rows(x, feven, fodd, wh, wl):
    rows, cols, chans = x.shape
    outs = wh.shape[-1]
    return pl.pallas_call(
        inner_kernel,
        in_specs=[VMEM] * 5,
        out_specs=VMEM,
        out_shape=jax.ShapeDtypeStruct((rows, cols, outs), F32),
        scratch_shapes=[
            pltpu.VMEM((rows * cols, chans), BF16),
            pltpu.VMEM((rows * cols, chans), BF16),
            pltpu.VMEM((3, rows * cols, outs), F32),
        ],
        name="inner_rows",
        compiler_params=PARAMS,
    )(x, feven, fodd, wh, wl)


def outer_kernel(reven_ref, rodd_ref, wh_ref, wl_ref, partial_ref, out_ref):
    step = pl.program_id(0)
    parity = lax.axis_index("row") % 2

    def finish(halo_ref):
        hi, lo = parts(halo_ref[...])
        taps = [dot3(hi, lo, wh_ref[0, dx], wl_ref[0, dx]) for dx in range(3)]
        out_ref[0] = jnp.maximum(partial_ref[0] + join_columns(*taps), 0.0)

    pl.when(step == parity)(lambda: finish(rodd_ref))
    pl.when(step != parity)(lambda: finish(reven_ref))


def outer_rows(partial, reven, rodd, wh, wl):
    rows, cols, outs = partial.shape
    row = pl.BlockSpec((1, cols, outs), lambda i: (i * (rows - 1), 0, 0))
    tap = pl.BlockSpec((1,) + wh.shape[1:], lambda i: (2 * i, 0, 0, 0))
    return pl.pallas_call(
        outer_kernel,
        grid=(2,),
        in_specs=[VMEM, VMEM, tap, tap, row],
        out_specs=row,
        out_shape=jax.ShapeDtypeStruct(partial.shape, F32),
        input_output_aliases={4: 0},
        name="outer_rows",
        compiler_params=PARAMS,
    )(reven, rodd, wh, wl, partial)


def local(features, conv_weight):
    frames, rows, cols, chans = features.shape
    field = features.reshape(rows, cols, chans)
    wh, wl = split_weights(conv_weight)
    for layer in range(conv_weight.shape[0]):
        peven, podd = pack_frames(field, chans // 8)
        feven, fodd = exchange(peven, "frame", 0), exchange(podd, "frame", 1)
        seven, sodd = edge_rows(field, feven, fodd)
        reven, rodd = exchange(seven, "row", 0), exchange(sodd, "row", 1)
        partial = inner_rows(field, feven, fodd, wh[layer], wl[layer])
        field = outer_rows(partial, reven, rodd, wh[layer], wl[layer])
    return field.reshape(features.shape)


def solution(mesh):
    placed = (P("frame", "row", None, None), P())
    return jax.shard_map(
        local, mesh=mesh, in_specs=placed, out_specs=P("frame", "row", None, None), check_vma=False
    )
```

```python
import functools

import jax
import jax.numpy as jnp
from jax import lax
from jax.experimental import pallas as pl
from jax.experimental.pallas import tpu as pltpu
from jax.sharding import PartitionSpec as P

F32 = jnp.float32
BF16 = jnp.bfloat16
VMEM = pl.BlockSpec(memory_space=pltpu.VMEM)
PARAMS = pltpu.CompilerParams(vmem_limit_bytes=40 * 2**20)
LANES = 128


def exchange(block, axis, odd):
    count = lax.axis_size(axis)
    pairs = [(i, i + 1) for i in range(odd, count - 1, 2)]
    return lax.ppermute(block, axis, pairs + [(b, a) for a, b in pairs])


def by_parity(axis, even_case, odd_case):
    parity = lax.axis_index(axis) % 2
    pl.when(parity == 0)(even_case)
    pl.when(parity == 1)(odd_case)


def parts(x):
    hi = x.astype(BF16)
    return hi, (x - hi.astype(F32)).astype(BF16)


def dot(a, b):
    return jnp.dot(a, b, preferred_element_type=F32)


def dot3(ah, al, bh, bl):
    return dot(ah, bh) + (dot(al, bh) + dot(ah, bl))


def lane_of(height):
    return lax.broadcasted_iota(jnp.int32, (height, LANES), 1)


def turn(x, lanes):
    return pltpu.roll(x, lanes % LANES, 1) if lanes % LANES else x


def shift_columns(x, dx):
    cols = x.shape[0]
    at = lax.broadcasted_iota(jnp.int32, x.shape, 0)
    if dx == 0:
        return jnp.where(at == 0, 0.0, pltpu.roll(x, 1, 0))
    if dx == 2:
        return jnp.where(at == cols - 1, 0.0, pltpu.roll(x, cols - 1, 0))
    return x


def pack(row, first, width):
    blocks = LANES // width
    height = row.shape[0] // blocks
    block = lane_of(height) // width
    out = turn(row[:height], -first)
    for j in range(1, blocks):
        out = jnp.where(block == j, turn(row[j * height : (j + 1) * height], j * width - first), out)
    return out


def shifted_lanes(own, following, before, fold):
    blocks = LANES // fold
    height = following.shape[0]
    lane = lane_of(height)
    pieces = []
    for j in range(blocks):
        nxt = turn(following, -j * fold)
        prv = turn(before, fold - j * fold)
        pieces.append(
            jnp.where(lane < fold, nxt, jnp.where(lane < 2 * fold, prv, own[j * height : (j + 1) * height]))
        )
    return jnp.concatenate(pieces, axis=0)


def shifted_packed(following, before, fold):
    halves = LANES // (2 * fold)
    block = lane_of(following.shape[0]) // fold
    pieces = []
    for i in range(halves):
        out = turn(following, -i * fold)
        for k in range(halves):
            j = k * halves + i
            out = jnp.where(block == 2 * k, turn(following, (2 * k - j) * fold), out)
            out = jnp.where(block == 2 * k + 1, turn(before, (2 * k + 1 - j) * fold), out)
        pieces.append(out)
    return jnp.concatenate(pieces, axis=0)


def send_kernel(fold, x_ref, fodd_ref, feven_ref, rodd_ref, reven_ref):
    rows, cols, chans = x_ref.shape

    def frames(to_before, to_following):
        for r in range(rows):
            lanes = x_ref[r, :, :LANES]
            to_before[r] = pack(lanes, 0, fold)
            to_following[r] = pack(lanes, fold, fold)

    def edges(first_to, last_to):
        for r, out in ((0, first_to), (rows - 1, last_to)):
            out[:cols] = x_ref[r, :, LANES:]
            out[cols:] = pack(x_ref[r, :, :LANES], 2 * fold, LANES - 2 * fold)

    by_parity("frame", lambda: frames(fodd_ref, feven_ref), lambda: frames(feven_ref, fodd_ref))
    by_parity("row", lambda: edges(rodd_ref, reven_ref), lambda: edges(reven_ref, rodd_ref))


def send(x):
    rows, cols, chans = x.shape
    fold = chans // 8
    frames = jax.ShapeDtypeStruct((rows, cols * fold // LANES, LANES), F32)
    edge = jax.ShapeDtypeStruct((cols * (chans - 2 * fold) // LANES, LANES), F32)
    return pl.pallas_call(
        functools.partial(send_kernel, fold),
        in_specs=[VMEM],
        out_specs=[VMEM] * 4,
        out_shape=[frames, frames, edge, edge],
        name="send",
        compiler_params=PARAMS,
    )(x)


def forward_kernel(fold, fodd_ref, feven_ref, sodd_ref, seven_ref):
    rows = fodd_ref.shape[0]

    def write(following, before, first_to, last_to):
        for r, out in ((0, first_to), (rows - 1, last_to)):
            out[...] = shifted_packed(following[r], before[r], fold)

    def rows_case(first_to, last_to):
        by_parity(
            "frame",
            lambda: write(feven_ref, fodd_ref, first_to, last_to),
            lambda: write(fodd_ref, feven_ref, first_to, last_to),
        )

    by_parity("row", lambda: rows_case(sodd_ref, seven_ref), lambda: rows_case(seven_ref, sodd_ref))


def forward(fodd, feven, cols, fold):
    edge = jax.ShapeDtypeStruct((cols * 2 * fold // LANES, LANES), F32)
    return pl.pallas_call(
        functools.partial(forward_kernel, fold),
        in_specs=[VMEM] * 2,
        out_specs=[VMEM] * 2,
        out_shape=[edge, edge],
        name="forward",
        compiler_params=PARAMS,
    )(fodd, feven)


def inner_kernel(fold, x_ref, fodd_ref, feven_ref, w_ref, out_ref, partial_ref, wh_ref, wl_ref, hi, lo):
    rows, cols, chans = x_ref.shape
    dx = pl.program_id(0)

    def write(following, before):
        for r in range(rows):
            lanes = shifted_lanes(x_ref[r, :, :LANES], following[r], before[r], fold)
            at = slice(r * cols, (r + 1) * cols)
            hi[at, :LANES], lo[at, :LANES] = parts(lanes)
            hi[at, LANES:], lo[at, LANES:] = parts(x_ref[r, :, LANES:])

    @pl.when(dx == 0)
    def _():
        by_parity("frame", lambda: write(feven_ref, fodd_ref), lambda: write(fodd_ref, feven_ref))

    weights = [parts(w_ref[0, dy, 0]) for dy in range(3)]
    for i, dy in enumerate((0, 2)):
        wh_ref[i, 0], wl_ref[i, 0] = weights[dy]

    def products(dy, first, last):
        at = slice(first * cols, last * cols)
        return dot3(hi[at], lo[at], *weights[dy])

    top = products(1, 0, 1) + products(2, 1, 2)
    middle = products(0, 0, rows - 2) + products(1, 1, rows - 1) + products(2, 2, rows)
    bottom = products(0, rows - 2, rows - 1) + products(1, rows - 1, rows)
    for k in range(3):

        @pl.when(dx == k)
        def _(k=k):
            for i, total in enumerate((top, bottom)):
                total = shift_columns(total, k)
                partial_ref[i] = total if k == 0 else partial_ref[i] + total
            for r in range(1, rows - 1):
                total = shift_columns(middle[(r - 1) * cols : r * cols], k)
                total = total if k == 0 else out_ref[r - 1] + total
                out_ref[r - 1] = jnp.maximum(total, 0.0) if k == 2 else total


def inner_rows(x, fodd, feven, weight, layer):
    rows, cols, chans = x.shape
    outs = weight.shape[-1]
    whole = lambda shape: pl.BlockSpec(shape, lambda dx: (0,) * len(shape))
    taps = pl.BlockSpec((2, 1, chans, outs), lambda dx: (0, dx, 0, 0))
    split = jax.ShapeDtypeStruct((2, 3, chans, outs), BF16)
    return pl.pallas_call(
        functools.partial(inner_kernel, chans // 8),
        grid=(3,),
        in_specs=[VMEM, VMEM, VMEM, pl.BlockSpec((1, 3, 1, chans, outs), lambda dx: (layer, 0, dx, 0, 0))],
        out_specs=[whole((rows - 2, cols, outs)), whole((2, cols, outs)), taps, taps],
        out_shape=[
            jax.ShapeDtypeStruct((rows - 2, cols, outs), F32),
            jax.ShapeDtypeStruct((2, cols, outs), F32),
            split,
            split,
        ],
        scratch_shapes=[pltpu.VMEM((rows * cols, chans), BF16), pltpu.VMEM((rows * cols, chans), BF16)],
        name="inner_rows",
        compiler_params=PARAMS,
    )(x, fodd, feven, weight)


def outer_kernel(fold, rodd_ref, reven_ref, sodd_ref, seven_ref, wh_ref, wl_ref, partial_ref, inner_ref, out_ref):
    rows, cols, outs = out_ref.shape
    width = 2 * fold
    out_ref[1 : rows - 1] = inner_ref[...]

    def finish(i, kept_ref, moved_ref):
        halves = LANES // width
        height = cols // halves
        lane = lane_of(height)
        low = []
        for k in range(halves):
            moved = turn(moved_ref[...], -k * width)
            kept = turn(kept_ref[cols:], width - k * width)
            low.append(jnp.where(lane < width, moved, kept))
        halo = jnp.concatenate([jnp.concatenate(low, axis=0), kept_ref[:cols]], axis=1)
        hi, lo = parts(halo)
        total = partial_ref[i]
        for dx in range(3):
            total = total + shift_columns(dot3(hi, lo, wh_ref[i, dx], wl_ref[i, dx]), dx)
        out_ref[i * (rows - 1)] = jnp.maximum(total, 0.0)

    def both(above, below):
        finish(0, *above)
        finish(1, *below)

    odd, even = (rodd_ref, sodd_ref), (reven_ref, seven_ref)
    by_parity("row", lambda: both(odd, even), lambda: both(even, odd))


def outer_rows(rodd, reven, sodd, seven, wh, wl, partial, inner):
    rows, cols, outs = inner.shape
    return pl.pallas_call(
        functools.partial(outer_kernel, wh.shape[2] // 8),
        in_specs=[VMEM] * 8,
        out_specs=VMEM,
        out_shape=jax.ShapeDtypeStruct((rows + 2, cols, outs), F32),
        name="outer_rows",
        compiler_params=PARAMS,
    )(rodd, reven, sodd, seven, wh, wl, partial, inner)


def local(features, conv_weight):
    frames, rows, cols, chans = features.shape
    field = features.reshape(rows, cols, chans)
    for layer in range(conv_weight.shape[0]):
        fodd, feven, rodd, reven = send(field)
        fodd, feven = exchange(fodd, "frame", 1), exchange(feven, "frame", 0)
        rodd, reven = exchange(rodd, "row", 1), exchange(reven, "row", 0)
        sodd, seven = forward(fodd, feven, cols, chans // 8)
        sodd, seven = exchange(sodd, "row", 1), exchange(seven, "row", 0)
        inner, partial, wh, wl = inner_rows(field, fodd, feven, conv_weight, layer)
        field = outer_rows(rodd, reven, sodd, seven, wh, wl, partial, inner)
    return field.reshape(features.shape)


def solution(mesh):
    placed = (P("frame", "row", None, None), P())
    return jax.shard_map(
        local, mesh=mesh, in_specs=placed, out_specs=P("frame", "row", None, None), check_vma=False
    )
```

```python
import functools

import jax
import jax.numpy as jnp
from jax import lax
from jax.experimental import pallas as pl
from jax.experimental.pallas import tpu as pltpu
from jax.sharding import PartitionSpec as P

F32 = jnp.float32
BF16 = jnp.bfloat16
VMEM = pl.BlockSpec(memory_space=pltpu.VMEM)
PARAMS = pltpu.CompilerParams(vmem_limit_bytes=40 * 2**20)
LANES = 128


def exchange(block, axis, odd):
    count = lax.axis_size(axis)
    pairs = [(i, i + 1) for i in range(odd, count - 1, 2)]
    return lax.ppermute(block, axis, pairs + [(b, a) for a, b in pairs])


def by_parity(axis, even_case, odd_case):
    parity = lax.axis_index(axis) % 2
    pl.when(parity == 0)(even_case)
    pl.when(parity == 1)(odd_case)


def parts(x):
    hi = x.astype(BF16)
    return hi, (x - hi.astype(F32)).astype(BF16)


def dot(a, b):
    return jnp.dot(a, b, preferred_element_type=F32)


def dot3(ah, al, bh, bl):
    return dot(ah, bh) + (dot(al, bh) + dot(ah, bl))


def lane_of(height):
    return lax.broadcasted_iota(jnp.int32, (height, LANES), 1)


def turn(x, lanes):
    return pltpu.roll(x, lanes % LANES, 1) if lanes % LANES else x


def shift_columns(x, dx):
    cols = x.shape[0]
    at = lax.broadcasted_iota(jnp.int32, x.shape, 0)
    if dx == 0:
        return jnp.where(at == 0, 0.0, pltpu.roll(x, 1, 0))
    if dx == 2:
        return jnp.where(at == cols - 1, 0.0, pltpu.roll(x, cols - 1, 0))
    return x


def pack(row, first, width):
    blocks = LANES // width
    height = row.shape[0] // blocks
    block = lane_of(height) // width
    out = turn(row[:height], -first)
    for j in range(1, blocks):
        out = jnp.where(block == j, turn(row[j * height : (j + 1) * height], j * width - first), out)
    return out


def shifted_lanes(own, following, before, fold):
    blocks = LANES // fold
    height = following.shape[0]
    lane = lane_of(height)
    pieces = []
    for j in range(blocks):
        nxt = turn(following, -j * fold)
        prv = turn(before, fold - j * fold)
        pieces.append(
            jnp.where(lane < fold, nxt, jnp.where(lane < 2 * fold, prv, own[j * height : (j + 1) * height]))
        )
    return jnp.concatenate(pieces, axis=0)


def shifted_packed(following, before, fold):
    halves = LANES // (2 * fold)
    block = lane_of(following.shape[0]) // fold
    pieces = []
    for i in range(halves):
        out = turn(following, -i * fold)
        for k in range(halves):
            j = k * halves + i
            out = jnp.where(block == 2 * k, turn(following, (2 * k - j) * fold), out)
            out = jnp.where(block == 2 * k + 1, turn(before, (2 * k + 1 - j) * fold), out)
        pieces.append(out)
    return jnp.concatenate(pieces, axis=0)


def send_kernel(fold, x_ref, fodd_ref, feven_ref, rodd_ref, reven_ref):
    rows, cols, chans = x_ref.shape

    def frames(to_before, to_following):
        for r in range(rows):
            lanes = x_ref[r, :, :LANES]
            to_before[r] = pack(lanes, 0, fold)
            to_following[r] = pack(lanes, fold, fold)

    def edges(first_to, last_to):
        for r, out in ((0, first_to), (rows - 1, last_to)):
            out[:cols] = x_ref[r, :, LANES:]
            out[cols:] = pack(x_ref[r, :, :LANES], 2 * fold, LANES - 2 * fold)

    by_parity("frame", lambda: frames(fodd_ref, feven_ref), lambda: frames(feven_ref, fodd_ref))
    by_parity("row", lambda: edges(rodd_ref, reven_ref), lambda: edges(reven_ref, rodd_ref))


def send(x):
    rows, cols, chans = x.shape
    fold = chans // 8
    frames = jax.ShapeDtypeStruct((rows, cols * fold // LANES, LANES), F32)
    edge = jax.ShapeDtypeStruct((cols * (chans - 2 * fold) // LANES, LANES), F32)
    return pl.pallas_call(
        functools.partial(send_kernel, fold),
        in_specs=[VMEM],
        out_specs=[VMEM] * 4,
        out_shape=[frames, frames, edge, edge],
        name="send",
        compiler_params=PARAMS,
    )(x)


def forward_kernel(fold, fodd_ref, feven_ref, ready_ref, sodd_ref, seven_ref):
    rows = fodd_ref.shape[0]

    def write(following, before, first_to, last_to):
        for r, out in ((0, first_to), (rows - 1, last_to)):
            out[...] = shifted_packed(following[r], before[r], fold)

    def rows_case(first_to, last_to):
        by_parity(
            "frame",
            lambda: write(feven_ref, fodd_ref, first_to, last_to),
            lambda: write(fodd_ref, feven_ref, first_to, last_to),
        )

    by_parity("row", lambda: rows_case(sodd_ref, seven_ref), lambda: rows_case(seven_ref, sodd_ref))


def forward(fodd, feven, ready, cols, fold):
    edge = jax.ShapeDtypeStruct((cols * 2 * fold // LANES, LANES), F32)
    return pl.pallas_call(
        functools.partial(forward_kernel, fold),
        in_specs=[VMEM] * 3,
        out_specs=[VMEM] * 2,
        out_shape=[edge, edge],
        name="forward",
        compiler_params=PARAMS,
    )(fodd, feven, ready)


def prepare_kernel(w_ref, *refs):
    layers = w_ref.shape[0]
    for l in range(layers):
        hi_ref, lo_ref = refs[2 * l], refs[2 * l + 1]
        for dx in range(3):
            first, mid, last = w_ref[l, 0, dx], w_ref[l, 1, dx], w_ref[l, 2, dx]
            ends = 0.5 * (first + last)
            half = 0.5 * mid
            for m, value in enumerate((first, ends + half, ends - half, last)):
                hi_ref[m, dx], lo_ref[m, dx] = parts(value)
    refs[2 * layers][...] = jnp.zeros_like(refs[2 * layers])


def prepare(weight):
    layers, _, _, chans, outs = weight.shape
    split = jax.ShapeDtypeStruct((4, 3, chans, outs), BF16)
    *split, ready = pl.pallas_call(
        prepare_kernel,
        in_specs=[VMEM],
        out_specs=[VMEM] * (2 * layers + 1),
        out_shape=[split] * (2 * layers) + [jax.ShapeDtypeStruct((8, LANES), F32)],
        name="prepare",
        compiler_params=PARAMS,
    )(weight)
    return split, ready


def inner_kernel(fold, x_ref, fodd_ref, feven_ref, wh_ref, wl_ref, out_ref, partial_ref, beside_ref, shifted, hi, lo):
    rows, cols, chans = x_ref.shape
    pairs = rows // 2

    def write(following, before):
        for r in range(rows):
            shifted[r, :, :LANES] = shifted_lanes(x_ref[r, :, :LANES], following[r], before[r], fold)
            shifted[r, :, LANES:] = x_ref[r, :, LANES:]

    by_parity("frame", lambda: write(feven_ref, fodd_ref), lambda: write(fodd_ref, feven_ref))
    beside_ref[0] = shifted[1]
    beside_ref[1] = shifted[rows - 2]

    def fill(at, value):
        place = slice(at * cols, (at + 1) * cols)
        hi[place], lo[place] = parts(value)

    for p in range(pairs):
        fill(p, shifted[2 * p] + shifted[2 * p + 1])
        fill(pairs + p, shifted[2 * p + 1] - shifted[2 * p])
    for p in range(pairs - 1):
        fill(2 * pairs + p, shifted[2 * p + 1] - shifted[2 * p + 3])
        fill(3 * pairs - 1 + p, shifted[2 * p] - shifted[2 * p + 2])

    def products(m, dx, first, count):
        at = slice(first * cols, (first + count) * cols)
        return dot3(hi[at], lo[at], wh_ref[m, dx], wl_ref[m, dx])

    totals = [None] * rows
    for dx in (1, 0, 2):
        plus = products(1, dx, 0, pairs)
        minus = products(2, dx, pairs, pairs)
        above = products(0, dx, 2 * pairs, pairs - 1)
        below = products(3, dx, 3 * pairs - 1, pairs - 1)
        for p in range(pairs):
            at = slice(p * cols, (p + 1) * cols)
            one = plus[at] + minus[at]
            if p > 0:
                one = one + above[(p - 1) * cols : p * cols]
            two = plus[at] - minus[at]
            if p < pairs - 1:
                two = two - below[p * cols : (p + 1) * cols]
            for r, value in ((2 * p, one), (2 * p + 1, two)):
                value = shift_columns(value, dx)
                totals[r] = value if totals[r] is None else totals[r] + value
    partial_ref[0] = totals[0]
    partial_ref[1] = totals[rows - 1]
    for r in range(1, rows - 1):
        out_ref[r - 1] = jnp.maximum(totals[r], 0.0)


def inner_rows(x, fodd, feven, wh, wl):
    rows, cols, chans = x.shape
    outs = wh.shape[-1]
    products = 4 * (rows // 2) - 2
    return pl.pallas_call(
        functools.partial(inner_kernel, chans // 8),
        in_specs=[VMEM] * 5,
        out_specs=[VMEM] * 3,
        out_shape=[
            jax.ShapeDtypeStruct((rows - 2, cols, outs), F32),
            jax.ShapeDtypeStruct((2, cols, outs), F32),
            jax.ShapeDtypeStruct((2, cols, chans), F32),
        ],
        scratch_shapes=[
            pltpu.VMEM((rows, cols, chans), F32),
            pltpu.VMEM((products * cols, chans), BF16),
            pltpu.VMEM((products * cols, chans), BF16),
        ],
        name="inner_rows",
        compiler_params=PARAMS,
    )(x, fodd, feven, wh, wl)


def outer_kernel(
    fold, rodd_ref, reven_ref, sodd_ref, seven_ref, wh_ref, wl_ref, partial_ref, beside_ref, inner_ref, out_ref
):
    rows, cols, outs = out_ref.shape
    width = 2 * fold
    out_ref[1 : rows - 1] = inner_ref[...]

    def finish(i, kept_ref, moved_ref):
        halves = LANES // width
        height = cols // halves
        lane = lane_of(height)
        low = []
        for k in range(halves):
            moved = turn(moved_ref[...], -k * width)
            kept = turn(kept_ref[cols:], width - k * width)
            low.append(jnp.where(lane < width, moved, kept))
        halo = jnp.concatenate([jnp.concatenate(low, axis=0), kept_ref[:cols]], axis=1)
        hi, lo = parts(halo - beside_ref[i])
        total = partial_ref[i]
        for dx in range(3):
            total = total + shift_columns(dot3(hi, lo, wh_ref[3 * i, dx], wl_ref[3 * i, dx]), dx)
        out_ref[i * (rows - 1)] = jnp.maximum(total, 0.0)

    def both(above, below):
        finish(0, *above)
        finish(1, *below)

    odd, even = (rodd_ref, sodd_ref), (reven_ref, seven_ref)
    by_parity("row", lambda: both(odd, even), lambda: both(even, odd))


def outer_rows(rodd, reven, sodd, seven, wh, wl, partial, beside, inner):
    rows, cols, outs = inner.shape
    return pl.pallas_call(
        functools.partial(outer_kernel, wh.shape[2] // 8),
        in_specs=[VMEM] * 9,
        out_specs=VMEM,
        out_shape=jax.ShapeDtypeStruct((rows + 2, cols, outs), F32),
        name="outer_rows",
        compiler_params=PARAMS,
    )(rodd, reven, sodd, seven, wh, wl, partial, beside, inner)


def local(features, conv_weight):
    frames, rows, cols, chans = features.shape
    field = features.reshape(rows, cols, chans)
    split, ready = prepare(conv_weight)
    for layer in range(conv_weight.shape[0]):
        wh, wl = split[2 * layer], split[2 * layer + 1]
        fodd, feven, rodd, reven = send(field)
        fodd, feven = exchange(fodd, "frame", 1), exchange(feven, "frame", 0)
        rodd, reven = exchange(rodd, "row", 1), exchange(reven, "row", 0)
        sodd, seven = forward(fodd, feven, ready, cols, chans // 8)
        sodd, seven = exchange(sodd, "row", 1), exchange(seven, "row", 0)
        inner, partial, beside = inner_rows(field, fodd, feven, wh, wl)
        field = outer_rows(rodd, reven, sodd, seven, wh, wl, partial, beside, inner)
    return field.reshape(features.shape)


def solution(mesh):
    placed = (P("frame", "row", None, None), P())
    return jax.shard_map(
        local, mesh=mesh, in_specs=placed, out_specs=P("frame", "row", None, None), check_vma=False
    )
```

```python
import functools

import jax
import jax.numpy as jnp
from jax import lax
from jax.experimental import pallas as pl
from jax.experimental.pallas import tpu as pltpu
from jax.sharding import PartitionSpec as P

F32 = jnp.float32
BF16 = jnp.bfloat16
VMEM = pl.BlockSpec(memory_space=pltpu.VMEM)
PARAMS = pltpu.CompilerParams(vmem_limit_bytes=40 * 2**20)
LANES = 128


def exchange(block, axis, odd):
    count = lax.axis_size(axis)
    pairs = [(i, i + 1) for i in range(odd, count - 1, 2)]
    return lax.ppermute(block, axis, pairs + [(b, a) for a, b in pairs])


def by_parity(axis, even_case, odd_case):
    parity = lax.axis_index(axis) % 2
    pl.when(parity == 0)(even_case)
    pl.when(parity == 1)(odd_case)


def parts(x):
    hi = x.astype(BF16)
    return hi, (x - hi.astype(F32)).astype(BF16)


def dot(a, b):
    return jnp.dot(a, b, preferred_element_type=F32)


def dot3(ah, al, bh, bl):
    return dot(ah, bh) + (dot(al, bh) + dot(ah, bl))


def lane_of(height):
    return lax.broadcasted_iota(jnp.int32, (height, LANES), 1)


def turn(x, lanes):
    return pltpu.roll(x, lanes % LANES, 1) if lanes % LANES else x


def shift_columns(x, dx):
    cols = x.shape[0]
    at = lax.broadcasted_iota(jnp.int32, x.shape, 0)
    if dx == 0:
        return jnp.where(at == 0, 0.0, pltpu.roll(x, 1, 0))
    if dx == 2:
        return jnp.where(at == cols - 1, 0.0, pltpu.roll(x, cols - 1, 0))
    return x


def pack(row, first, width):
    blocks = LANES // width
    height = row.shape[0] // blocks
    block = lane_of(height) // width
    out = turn(row[:height], -first)
    for j in range(1, blocks):
        out = jnp.where(block == j, turn(row[j * height : (j + 1) * height], j * width - first), out)
    return out


def shifted_lanes(own, following, before, fold):
    blocks = LANES // fold
    height = following.shape[0]
    lane = lane_of(height)
    pieces = []
    for j in range(blocks):
        nxt = turn(following, -j * fold)
        prv = turn(before, fold - j * fold)
        pieces.append(
            jnp.where(lane < fold, nxt, jnp.where(lane < 2 * fold, prv, own[j * height : (j + 1) * height]))
        )
    return jnp.concatenate(pieces, axis=0)


def shifted_packed(following, before, fold):
    halves = LANES // (2 * fold)
    block = lane_of(following.shape[0]) // fold
    pieces = []
    for i in range(halves):
        out = turn(following, -i * fold)
        for k in range(halves):
            j = k * halves + i
            out = jnp.where(block == 2 * k, turn(following, (2 * k - j) * fold), out)
            out = jnp.where(block == 2 * k + 1, turn(before, (2 * k + 1 - j) * fold), out)
        pieces.append(out)
    return jnp.concatenate(pieces, axis=0)


def frames_kernel(fold, x_ref, even_ref, odd_ref):
    def write(to_before, to_following):
        for r in range(x_ref.shape[0]):
            lanes = x_ref[r, :, :LANES]
            to_before[r] = pack(lanes, 0, fold)
            to_following[r] = pack(lanes, fold, fold)

    by_parity("frame", lambda: write(odd_ref, even_ref), lambda: write(even_ref, odd_ref))


def frames_to_send(x):
    rows, cols, chans = x.shape
    fold = chans // 8
    frames = jax.ShapeDtypeStruct((rows, cols * fold // LANES, LANES), F32)
    return pl.pallas_call(
        functools.partial(frames_kernel, fold),
        in_specs=[VMEM],
        out_specs=[VMEM] * 2,
        out_shape=[frames, frames],
        name="frames_to_send",
        compiler_params=PARAMS,
    )(x)


def rows_kernel(fold, x_ref, even_ref, odd_ref):
    rows, cols, chans = x_ref.shape

    def write(first_to, last_to):
        for r, out in ((0, first_to), (rows - 1, last_to)):
            out[:cols] = x_ref[r, :, LANES:]
            out[cols:] = pack(x_ref[r, :, :LANES], 2 * fold, LANES - 2 * fold)

    by_parity("row", lambda: write(odd_ref, even_ref), lambda: write(even_ref, odd_ref))


def rows_to_send(x):
    rows, cols, chans = x.shape
    fold = chans // 8
    edge = jax.ShapeDtypeStruct((cols * (chans - 2 * fold) // LANES, LANES), F32)
    return pl.pallas_call(
        functools.partial(rows_kernel, fold),
        in_specs=[VMEM],
        out_specs=[VMEM] * 2,
        out_shape=[edge, edge],
        name="rows_to_send",
        compiler_params=PARAMS,
    )(x)


def forward_kernel(fold, feven_ref, fodd_ref, ready_ref, sodd_ref, seven_ref):
    rows = fodd_ref.shape[0]

    def write(following, before, first_to, last_to):
        for r, out in ((0, first_to), (rows - 1, last_to)):
            out[...] = shifted_packed(following[r], before[r], fold)

    def rows_case(first_to, last_to):
        by_parity(
            "frame",
            lambda: write(feven_ref, fodd_ref, first_to, last_to),
            lambda: write(fodd_ref, feven_ref, first_to, last_to),
        )

    by_parity("row", lambda: rows_case(sodd_ref, seven_ref), lambda: rows_case(seven_ref, sodd_ref))


def forward(fodd, feven, ready, cols, fold):
    edge = jax.ShapeDtypeStruct((cols * 2 * fold // LANES, LANES), F32)
    return pl.pallas_call(
        functools.partial(forward_kernel, fold),
        in_specs=[VMEM] * 3,
        out_specs=[VMEM] * 2,
        out_shape=[edge, edge],
        name="forward",
        compiler_params=PARAMS,
    )(feven, fodd, ready)


def prepare_kernel(w_ref, *refs):
    layers = w_ref.shape[0]
    outs, (stage, sems) = refs[: 2 * layers + 1], refs[2 * layers + 1 :]
    order = [(l, dx) for l in range(layers) for dx in range(3)]
    copies = [pltpu.make_async_copy(w_ref.at[l, :, dx], stage.at[l, dx], sems.at[l, dx]) for l, dx in order]
    for copy in copies:
        copy.start()
    for (l, dx), copy in zip(order, copies):
        copy.wait()
        first, mid, last = stage[l, dx, 0], stage[l, dx, 1], stage[l, dx, 2]
        ends = 0.5 * (first + last)
        half = 0.5 * mid
        for m, value in enumerate((first, ends + half, ends - half, last)):
            outs[2 * l][m, dx], outs[2 * l + 1][m, dx] = parts(value)
    outs[2 * layers][...] = jnp.zeros_like(outs[2 * layers])


def prepare(weight):
    layers, _, _, chans, outs = weight.shape
    split = jax.ShapeDtypeStruct((4, 3, chans, outs), BF16)
    *split, ready = pl.pallas_call(
        prepare_kernel,
        in_specs=[pl.BlockSpec(memory_space=pltpu.HBM)],
        out_specs=[VMEM] * (2 * layers + 1),
        out_shape=[split] * (2 * layers) + [jax.ShapeDtypeStruct((8, LANES), F32)],
        scratch_shapes=[
            pltpu.VMEM((layers, 3, 3, chans, outs), F32),
            pltpu.SemaphoreType.DMA((layers, 3)),
        ],
        name="prepare",
        compiler_params=pltpu.CompilerParams(vmem_limit_bytes=46 * 2**20),
    )(weight)
    return split, ready


def inner_kernel(fold, x_ref, feven_ref, fodd_ref, wh_ref, wl_ref, out_ref, partial_ref, beside_ref, shifted, hi, lo):
    rows, cols, chans = x_ref.shape
    pairs = rows // 2

    def write(following, before):
        for r in range(rows):
            shifted[r, :, :LANES] = shifted_lanes(x_ref[r, :, :LANES], following[r], before[r], fold)
            shifted[r, :, LANES:] = x_ref[r, :, LANES:]

    by_parity("frame", lambda: write(feven_ref, fodd_ref), lambda: write(fodd_ref, feven_ref))
    beside_ref[0] = shifted[1]
    beside_ref[1] = shifted[rows - 2]

    def fill(at, value):
        place = slice(at * cols, (at + 1) * cols)
        hi[place], lo[place] = parts(value)

    for p in range(pairs):
        fill(p, shifted[2 * p] + shifted[2 * p + 1])
        fill(pairs + p, shifted[2 * p + 1] - shifted[2 * p])
    for p in range(pairs - 1):
        fill(2 * pairs + p, shifted[2 * p + 1] - shifted[2 * p + 3])
        fill(3 * pairs - 1 + p, shifted[2 * p] - shifted[2 * p + 2])

    def products(m, dx, first, count):
        at = slice(first * cols, (first + count) * cols)
        return dot3(hi[at], lo[at], wh_ref[m, dx], wl_ref[m, dx])

    totals = [None] * rows
    for dx in (1, 0, 2):
        plus = products(1, dx, 0, pairs)
        minus = products(2, dx, pairs, pairs)
        above = products(0, dx, 2 * pairs, pairs - 1)
        below = products(3, dx, 3 * pairs - 1, pairs - 1)
        for p in range(pairs):
            at = slice(p * cols, (p + 1) * cols)
            one = plus[at] + minus[at]
            if p > 0:
                one = one + above[(p - 1) * cols : p * cols]
            two = plus[at] - minus[at]
            if p < pairs - 1:
                two = two - below[p * cols : (p + 1) * cols]
            for r, value in ((2 * p, one), (2 * p + 1, two)):
                value = shift_columns(value, dx)
                totals[r] = value if totals[r] is None else totals[r] + value
    partial_ref[0] = totals[0]
    partial_ref[1] = totals[rows - 1]
    for r in range(1, rows - 1):
        out_ref[r - 1] = jnp.maximum(totals[r], 0.0)


def inner_rows(x, fodd, feven, wh, wl):
    rows, cols, chans = x.shape
    outs = wh.shape[-1]
    products = 4 * (rows // 2) - 2
    return pl.pallas_call(
        functools.partial(inner_kernel, chans // 8),
        in_specs=[VMEM] * 5,
        out_specs=[VMEM] * 3,
        out_shape=[
            jax.ShapeDtypeStruct((rows - 2, cols, outs), F32),
            jax.ShapeDtypeStruct((2, cols, outs), F32),
            jax.ShapeDtypeStruct((2, cols, chans), F32),
        ],
        scratch_shapes=[
            pltpu.VMEM((rows, cols, chans), F32),
            pltpu.VMEM((products * cols, chans), BF16),
            pltpu.VMEM((products * cols, chans), BF16),
        ],
        name="inner_rows",
        compiler_params=PARAMS,
    )(x, feven, fodd, wh, wl)


def outer_kernel(
    fold, reven_ref, rodd_ref, sodd_ref, seven_ref, wh_ref, wl_ref, partial_ref, beside_ref, inner_ref, out_ref, *scratch
):
    rows, cols, outs = out_ref.shape
    width = 2 * fold
    edges = (0, rows - 1)
    if scratch:
        stage, sems = scratch
        copies = [pltpu.make_async_copy(stage.at[i], out_ref.at[r], sems.at[i]) for i, r in enumerate(edges)]
        copies.append(pltpu.make_async_copy(inner_ref, out_ref.at[1 : rows - 1], sems.at[2]))
        copies[2].start()
    else:
        out_ref[1 : rows - 1] = inner_ref[...]

    def finish(i, kept_ref, moved_ref):
        halves = LANES // width
        height = cols // halves
        lane = lane_of(height)
        low = []
        for k in range(halves):
            moved = turn(moved_ref[...], -k * width)
            kept = turn(kept_ref[cols:], width - k * width)
            low.append(jnp.where(lane < width, moved, kept))
        halo = jnp.concatenate([jnp.concatenate(low, axis=0), kept_ref[:cols]], axis=1)
        hi, lo = parts(halo - beside_ref[i])
        total = partial_ref[i]
        for dx in range(3):
            total = total + shift_columns(dot3(hi, lo, wh_ref[3 * i, dx], wl_ref[3 * i, dx]), dx)
        total = jnp.maximum(total, 0.0)
        if scratch:
            stage[i] = total
            copies[i].start()
        else:
            out_ref[edges[i]] = total

    def both(above, below):
        finish(0, *above)
        finish(1, *below)

    odd, even = (rodd_ref, sodd_ref), (reven_ref, seven_ref)
    by_parity("row", lambda: both(odd, even), lambda: both(even, odd))
    if scratch:
        for copy in copies:
            copy.wait()


def outer_rows(reven, rodd, sodd, seven, wh, wl, partial, beside, inner, resident):
    rows, cols, outs = inner.shape
    stage = [pltpu.VMEM((2, cols, outs), F32), pltpu.SemaphoreType.DMA((3,))]
    return pl.pallas_call(
        functools.partial(outer_kernel, wh.shape[2] // 8),
        in_specs=[VMEM] * 9,
        out_specs=VMEM if resident else pl.BlockSpec(memory_space=pltpu.HBM),
        out_shape=jax.ShapeDtypeStruct((rows + 2, cols, outs), F32),
        scratch_shapes=[] if resident else stage,
        name="outer_rows",
        compiler_params=PARAMS,
    )(reven, rodd, sodd, seven, wh, wl, partial, beside, inner)


def local(features, conv_weight):
    frames, rows, cols, chans = features.shape
    layers = conv_weight.shape[0]
    field = features.reshape(rows, cols, chans)
    split, ready = prepare(conv_weight)
    for layer in range(layers):
        wh, wl = split[2 * layer], split[2 * layer + 1]
        feven, fodd = frames_to_send(field)
        feven, fodd = exchange(feven, "frame", 0), exchange(fodd, "frame", 1)
        reven, rodd = rows_to_send(field)
        reven, rodd = exchange(reven, "row", 0), exchange(rodd, "row", 1)
        sodd, seven = forward(fodd, feven, ready, cols, chans // 8)
        sodd, seven = exchange(sodd, "row", 1), exchange(seven, "row", 0)
        inner, partial, beside = inner_rows(field, fodd, feven, wh, wl)
        field = outer_rows(reven, rodd, sodd, seven, wh, wl, partial, beside, inner, layer < layers - 1)
    return field.reshape(features.shape)


def solution(mesh):
    placed = (P("frame", "row", None, None), P())
    return jax.shard_map(
        local, mesh=mesh, in_specs=placed, out_specs=P("frame", "row", None, None), check_vma=False
    )
```

```python
import functools

import jax
import jax.numpy as jnp
from jax import lax
from jax.experimental import pallas as pl
from jax.experimental.pallas import tpu as pltpu
from jax.sharding import PartitionSpec as P

F32 = jnp.float32
BF16 = jnp.bfloat16
VMEM = pl.BlockSpec(memory_space=pltpu.VMEM)
PARAMS = pltpu.CompilerParams(vmem_limit_bytes=40 * 2**20)
LANES = 128


def exchange(block, axis, odd):
    count = lax.axis_size(axis)
    pairs = [(i, i + 1) for i in range(odd, count - 1, 2)]
    return lax.ppermute(block, axis, pairs + [(b, a) for a, b in pairs])


def by_parity(axis, even_case, odd_case):
    parity = lax.axis_index(axis) % 2
    pl.when(parity == 0)(even_case)
    pl.when(parity == 1)(odd_case)


def parts(x):
    hi = x.astype(BF16)
    return hi, (x - hi.astype(F32)).astype(BF16)


def dot(a, b):
    return jnp.dot(a, b, preferred_element_type=F32)


def dot3(ah, al, bh, bl):
    return dot(ah, bh) + (dot(al, bh) + dot(ah, bl))


def lane_of(height):
    return lax.broadcasted_iota(jnp.int32, (height, LANES), 1)


def turn(x, lanes):
    return pltpu.roll(x, lanes % LANES, 1) if lanes % LANES else x


def shift_columns(x, dx):
    cols = x.shape[0]
    at = lax.broadcasted_iota(jnp.int32, x.shape, 0)
    if dx == 0:
        return jnp.where(at == 0, 0.0, pltpu.roll(x, 1, 0))
    if dx == 2:
        return jnp.where(at == cols - 1, 0.0, pltpu.roll(x, cols - 1, 0))
    return x


def pack(row, first, width):
    blocks = LANES // width
    height = row.shape[0] // blocks
    block = lane_of(height) // width
    out = turn(row[:height], -first)
    for j in range(1, blocks):
        out = jnp.where(block == j, turn(row[j * height : (j + 1) * height], j * width - first), out)
    return out


def shifted_lanes(own, following, before, fold):
    blocks = LANES // fold
    height = following.shape[0]
    lane = lane_of(height)
    pieces = []
    for j in range(blocks):
        nxt = turn(following, -j * fold)
        prv = turn(before, fold - j * fold)
        pieces.append(
            jnp.where(lane < fold, nxt, jnp.where(lane < 2 * fold, prv, own[j * height : (j + 1) * height]))
        )
    return jnp.concatenate(pieces, axis=0)


def shifted_packed(following, before, fold):
    halves = LANES // (2 * fold)
    block = lane_of(following.shape[0]) // fold
    pieces = []
    for i in range(halves):
        out = turn(following, -i * fold)
        for k in range(halves):
            j = k * halves + i
            out = jnp.where(block == 2 * k, turn(following, (2 * k - j) * fold), out)
            out = jnp.where(block == 2 * k + 1, turn(before, (2 * k + 1 - j) * fold), out)
        pieces.append(out)
    return jnp.concatenate(pieces, axis=0)


def frames_kernel(fold, x_ref, even_ref, odd_ref):
    def write(to_before, to_following):
        for r in range(x_ref.shape[0]):
            lanes = x_ref[r, :, :LANES]
            to_before[r] = pack(lanes, 0, fold)
            to_following[r] = pack(lanes, fold, fold)

    by_parity("frame", lambda: write(odd_ref, even_ref), lambda: write(even_ref, odd_ref))


def frames_to_send(x, fold):
    rows, cols, _ = x.shape
    frames = jax.ShapeDtypeStruct((rows, cols * fold // LANES, LANES), F32)
    return pl.pallas_call(
        functools.partial(frames_kernel, fold),
        in_specs=[VMEM],
        out_specs=[VMEM] * 2,
        out_shape=[frames, frames],
        name="frames_to_send",
        compiler_params=PARAMS,
    )(x)


def rows_kernel(fold, x_ref, even_ref, odd_ref):
    rows, cols, chans = x_ref.shape

    def write(first_to, last_to):
        for r, out in ((0, first_to), (rows - 1, last_to)):
            out[:cols] = x_ref[r, :, LANES:]
            out[cols:] = pack(x_ref[r, :, :LANES], 2 * fold, LANES - 2 * fold)

    by_parity("row", lambda: write(odd_ref, even_ref), lambda: write(even_ref, odd_ref))


def rows_to_send(x):
    rows, cols, chans = x.shape
    fold = chans // 8
    edge = jax.ShapeDtypeStruct((cols * (chans - 2 * fold) // LANES, LANES), F32)
    return pl.pallas_call(
        functools.partial(rows_kernel, fold),
        in_specs=[VMEM],
        out_specs=[VMEM] * 2,
        out_shape=[edge, edge],
        name="rows_to_send",
        compiler_params=PARAMS,
    )(x)


def forward_kernel(fold, feven_ref, fodd_ref, ready_ref, sodd_ref, seven_ref):
    rows = fodd_ref.shape[0]

    def write(following, before, first_to, last_to):
        for r, out in ((0, first_to), (rows - 1, last_to)):
            out[...] = shifted_packed(following[r], before[r], fold)

    def rows_case(first_to, last_to):
        by_parity(
            "frame",
            lambda: write(feven_ref, fodd_ref, first_to, last_to),
            lambda: write(fodd_ref, feven_ref, first_to, last_to),
        )

    by_parity("row", lambda: rows_case(sodd_ref, seven_ref), lambda: rows_case(seven_ref, sodd_ref))


def forward(fodd, feven, ready, cols, fold):
    edge = jax.ShapeDtypeStruct((cols * 2 * fold // LANES, LANES), F32)
    return pl.pallas_call(
        functools.partial(forward_kernel, fold),
        in_specs=[VMEM] * 3,
        out_specs=[VMEM] * 2,
        out_shape=[edge, edge],
        name="forward",
        compiler_params=PARAMS,
    )(feven, fodd, ready)


def prepare_kernel(layer, w_ref, after_ref, hi_ref, lo_ref, ready_ref, stage, sems):
    copies = [pltpu.make_async_copy(w_ref.at[layer, :, dx], stage.at[dx], sems.at[dx]) for dx in range(3)]
    for copy in copies:
        copy.start()
    for dx, copy in enumerate(copies):
        copy.wait()
        first, mid, last = stage[dx, 0], stage[dx, 1], stage[dx, 2]
        ends = 0.5 * (first + last)
        half = 0.5 * mid
        for m, value in enumerate((first, ends + half, ends - half, last)):
            hi_ref[m, dx], lo_ref[m, dx] = parts(value)
    ready_ref[...] = jnp.zeros_like(ready_ref)


def prepare(weight, layer, after):
    _, _, _, chans, outs = weight.shape
    split = jax.ShapeDtypeStruct((4, 3, chans, outs), BF16)
    return pl.pallas_call(
        functools.partial(prepare_kernel, layer),
        in_specs=[pl.BlockSpec(memory_space=pltpu.HBM), VMEM],
        out_specs=[VMEM] * 3,
        out_shape=[split, split, jax.ShapeDtypeStruct((8, LANES), F32)],
        scratch_shapes=[pltpu.VMEM((3, 3, chans, outs), F32), pltpu.SemaphoreType.DMA((3,))],
        name="prepare",
        compiler_params=pltpu.CompilerParams(vmem_limit_bytes=49 * 2**20),
    )(weight, after)


def inner_kernel(fold, x_ref, feven_ref, fodd_ref, wh_ref, wl_ref, out_ref, partial_ref, beside_ref, shifted, hi, lo):
    rows, cols, chans = x_ref.shape
    pairs = rows // 2

    def write(following, before):
        for r in range(rows):
            shifted[r, :, :LANES] = shifted_lanes(x_ref[r, :, :LANES], following[r], before[r], fold)
            shifted[r, :, LANES:] = x_ref[r, :, LANES:]

    by_parity("frame", lambda: write(feven_ref, fodd_ref), lambda: write(fodd_ref, feven_ref))
    beside_ref[0] = shifted[1]
    beside_ref[1] = shifted[rows - 2]

    def fill(at, value):
        place = slice(at * cols, (at + 1) * cols)
        hi[place], lo[place] = parts(value)

    for p in range(pairs):
        fill(p, shifted[2 * p] + shifted[2 * p + 1])
        fill(pairs + p, shifted[2 * p + 1] - shifted[2 * p])
    for p in range(pairs - 1):
        fill(2 * pairs + p, shifted[2 * p + 1] - shifted[2 * p + 3])
        fill(3 * pairs - 1 + p, shifted[2 * p] - shifted[2 * p + 2])

    def products(m, dx, first, count):
        at = slice(first * cols, (first + count) * cols)
        return dot3(hi[at], lo[at], wh_ref[m, dx], wl_ref[m, dx])

    totals = [None] * rows
    for dx in (1, 0, 2):
        plus = products(1, dx, 0, pairs)
        minus = products(2, dx, pairs, pairs)
        above = products(0, dx, 2 * pairs, pairs - 1)
        below = products(3, dx, 3 * pairs - 1, pairs - 1)
        for p in range(pairs):
            at = slice(p * cols, (p + 1) * cols)
            one = plus[at] + minus[at]
            if p > 0:
                one = one + above[(p - 1) * cols : p * cols]
            two = plus[at] - minus[at]
            if p < pairs - 1:
                two = two - below[p * cols : (p + 1) * cols]
            for r, value in ((2 * p, one), (2 * p + 1, two)):
                value = shift_columns(value, dx)
                totals[r] = value if totals[r] is None else totals[r] + value
    partial_ref[0] = totals[0]
    partial_ref[1] = totals[rows - 1]
    for r in range(1, rows - 1):
        out_ref[r - 1] = jnp.maximum(totals[r], 0.0)


def inner_rows(x, fodd, feven, wh, wl):
    rows, cols, chans = x.shape
    outs = wh.shape[-1]
    products = 4 * (rows // 2) - 2
    return pl.pallas_call(
        functools.partial(inner_kernel, chans // 8),
        in_specs=[VMEM] * 5,
        out_specs=[VMEM] * 3,
        out_shape=[
            jax.ShapeDtypeStruct((rows - 2, cols, outs), F32),
            jax.ShapeDtypeStruct((2, cols, outs), F32),
            jax.ShapeDtypeStruct((2, cols, chans), F32),
        ],
        scratch_shapes=[
            pltpu.VMEM((rows, cols, chans), F32),
            pltpu.VMEM((products * cols, chans), BF16),
            pltpu.VMEM((products * cols, chans), BF16),
        ],
        name="inner_rows",
        compiler_params=PARAMS,
    )(x, feven, fodd, wh, wl)


def outer_kernel(
    fold, reven_ref, rodd_ref, sodd_ref, seven_ref, wh_ref, wl_ref, partial_ref, beside_ref, inner_ref, out_ref, *scratch
):
    rows, cols, outs = out_ref.shape
    width = 2 * fold
    edges = (0, rows - 1)
    if scratch:
        stage, sems = scratch
        copies = [pltpu.make_async_copy(stage.at[i], out_ref.at[r], sems.at[i]) for i, r in enumerate(edges)]
        copies.append(pltpu.make_async_copy(inner_ref, out_ref.at[1 : rows - 1], sems.at[2]))
        copies[2].start()
    else:
        out_ref[1 : rows - 1] = inner_ref[...]

    def finish(i, kept_ref, moved_ref):
        halves = LANES // width
        height = cols // halves
        lane = lane_of(height)
        low = []
        for k in range(halves):
            moved = turn(moved_ref[...], -k * width)
            kept = turn(kept_ref[cols:], width - k * width)
            low.append(jnp.where(lane < width, moved, kept))
        halo = jnp.concatenate([jnp.concatenate(low, axis=0), kept_ref[:cols]], axis=1)
        hi, lo = parts(halo - beside_ref[i])
        total = partial_ref[i]
        for dx in range(3):
            total = total + shift_columns(dot3(hi, lo, wh_ref[3 * i, dx], wl_ref[3 * i, dx]), dx)
        total = jnp.maximum(total, 0.0)
        if scratch:
            stage[i] = total
            copies[i].start()
        else:
            out_ref[edges[i]] = total

    def both(above, below):
        finish(0, *above)
        finish(1, *below)

    odd, even = (rodd_ref, sodd_ref), (reven_ref, seven_ref)
    by_parity("row", lambda: both(odd, even), lambda: both(even, odd))
    if scratch:
        for copy in copies:
            copy.wait()


def outer_rows(reven, rodd, sodd, seven, wh, wl, partial, beside, inner, resident):
    rows, cols, outs = inner.shape
    stage = [pltpu.VMEM((2, cols, outs), F32), pltpu.SemaphoreType.DMA((3,))]
    return pl.pallas_call(
        functools.partial(outer_kernel, wh.shape[2] // 8),
        in_specs=[VMEM] * 9,
        out_specs=VMEM if resident else pl.BlockSpec(memory_space=pltpu.HBM),
        out_shape=jax.ShapeDtypeStruct((rows + 2, cols, outs), F32),
        scratch_shapes=[] if resident else stage,
        name="outer_rows",
        compiler_params=PARAMS,
    )(reven, rodd, sodd, seven, wh, wl, partial, beside, inner)


def local(features, conv_weight):
    frames, rows, cols, chans = features.shape
    layers = conv_weight.shape[0]
    field = features.reshape(rows, cols, chans)
    for layer in range(layers):
        feven, fodd = frames_to_send(field if layer else lax.slice_in_dim(field, 0, LANES, axis=2), chans // 8)
        feven, fodd = exchange(feven, "frame", 0), exchange(fodd, "frame", 1)
        wh, wl, ready = prepare(conv_weight, layer, feven)
        reven, rodd = rows_to_send(field)
        reven, rodd = exchange(reven, "row", 0), exchange(rodd, "row", 1)
        sodd, seven = forward(fodd, feven, ready, cols, chans // 8)
        sodd, seven = exchange(sodd, "row", 1), exchange(seven, "row", 0)
        inner, partial, beside = inner_rows(field, fodd, feven, wh, wl)
        field = outer_rows(reven, rodd, sodd, seven, wh, wl, partial, beside, inner, layer < layers - 1)
    return field.reshape(features.shape)


def solution(mesh):
    placed = (P("frame", "row", None, None), P())
    return jax.shard_map(
        local, mesh=mesh, in_specs=placed, out_specs=P("frame", "row", None, None), check_vma=False
    )
```

```python
import functools

import jax
import jax.numpy as jnp
from jax import lax
from jax.experimental import pallas as pl
from jax.experimental.pallas import tpu as pltpu
from jax.sharding import PartitionSpec as P

F32 = jnp.float32
BF16 = jnp.bfloat16
VMEM = pl.BlockSpec(memory_space=pltpu.VMEM)
PARAMS = pltpu.CompilerParams(vmem_limit_bytes=40 * 2**20)
LANES = 128


def exchange(block, axis, odd):
    count = lax.axis_size(axis)
    pairs = [(i, i + 1) for i in range(odd, count - 1, 2)]
    return lax.ppermute(block, axis, pairs + [(b, a) for a, b in pairs])


def by_parity(axis, even_case, odd_case):
    parity = lax.axis_index(axis) % 2
    pl.when(parity == 0)(even_case)
    pl.when(parity == 1)(odd_case)


def parts(x):
    hi = x.astype(BF16)
    return hi, (x - hi.astype(F32)).astype(BF16)


def dot(a, b):
    return jnp.dot(a, b, preferred_element_type=F32)


def dot3(ah, al, bh, bl):
    return dot(ah, bh) + (dot(al, bh) + dot(ah, bl))


def lane_of(height):
    return lax.broadcasted_iota(jnp.int32, (height, LANES), 1)


def turn(x, lanes):
    return pltpu.roll(x, lanes % LANES, 1) if lanes % LANES else x


def shift_columns(x, dx):
    cols = x.shape[0]
    at = lax.broadcasted_iota(jnp.int32, x.shape, 0)
    if dx == 0:
        return jnp.where(at == 0, 0.0, pltpu.roll(x, 1, 0))
    if dx == 2:
        return jnp.where(at == cols - 1, 0.0, pltpu.roll(x, cols - 1, 0))
    return x


def pack(row, first, width):
    blocks = LANES // width
    height = row.shape[0] // blocks
    block = lane_of(height) // width
    out = turn(row[:height], -first)
    for j in range(1, blocks):
        out = jnp.where(block == j, turn(row[j * height : (j + 1) * height], j * width - first), out)
    return out


def shifted_lanes(own, following, before, fold):
    blocks = LANES // fold
    height = following.shape[0]
    lane = lane_of(height)
    pieces = []
    for j in range(blocks):
        nxt = turn(following, -j * fold)
        prv = turn(before, fold - j * fold)
        pieces.append(
            jnp.where(lane < fold, nxt, jnp.where(lane < 2 * fold, prv, own[j * height : (j + 1) * height]))
        )
    return jnp.concatenate(pieces, axis=0)


def shifted_packed(following, before, fold):
    halves = LANES // (2 * fold)
    block = lane_of(following.shape[0]) // fold
    pieces = []
    for i in range(halves):
        out = turn(following, -i * fold)
        for k in range(halves):
            j = k * halves + i
            out = jnp.where(block == 2 * k, turn(following, (2 * k - j) * fold), out)
            out = jnp.where(block == 2 * k + 1, turn(before, (2 * k + 1 - j) * fold), out)
        pieces.append(out)
    return jnp.concatenate(pieces, axis=0)


def frames_kernel(fold, x_ref, even_ref, odd_ref):
    def write(to_before, to_following):
        for r in range(x_ref.shape[0]):
            lanes = x_ref[r, :, :LANES]
            to_before[r] = pack(lanes, 0, fold)
            to_following[r] = pack(lanes, fold, fold)

    by_parity("frame", lambda: write(odd_ref, even_ref), lambda: write(even_ref, odd_ref))


def frames_to_send(x, fold):
    rows, cols, _ = x.shape
    frames = jax.ShapeDtypeStruct((rows, cols * fold // LANES, LANES), F32)
    return pl.pallas_call(
        functools.partial(frames_kernel, fold),
        in_specs=[VMEM],
        out_specs=[VMEM] * 2,
        out_shape=[frames, frames],
        name="frames_to_send",
        compiler_params=PARAMS,
    )(x)


def rows_kernel(fold, x_ref, even_ref, odd_ref):
    rows, cols, chans = x_ref.shape

    def write(first_to, last_to):
        for r, out in ((0, first_to), (rows - 1, last_to)):
            out[:cols] = x_ref[r, :, LANES:]
            out[cols:] = pack(x_ref[r, :, :LANES], 2 * fold, LANES - 2 * fold)

    by_parity("row", lambda: write(odd_ref, even_ref), lambda: write(even_ref, odd_ref))


def rows_to_send(x):
    rows, cols, chans = x.shape
    fold = chans // 8
    edge = jax.ShapeDtypeStruct((cols * (chans - 2 * fold) // LANES, LANES), F32)
    return pl.pallas_call(
        functools.partial(rows_kernel, fold),
        in_specs=[VMEM],
        out_specs=[VMEM] * 2,
        out_shape=[edge, edge],
        name="rows_to_send",
        compiler_params=PARAMS,
    )(x)


def forward_kernel(fold, feven_ref, fodd_ref, ready_ref, sodd_ref, seven_ref):
    rows = fodd_ref.shape[0]

    def write(following, before, first_to, last_to):
        for r, out in ((0, first_to), (rows - 1, last_to)):
            out[...] = shifted_packed(following[r], before[r], fold)

    def rows_case(first_to, last_to):
        by_parity(
            "frame",
            lambda: write(feven_ref, fodd_ref, first_to, last_to),
            lambda: write(fodd_ref, feven_ref, first_to, last_to),
        )

    by_parity("row", lambda: rows_case(sodd_ref, seven_ref), lambda: rows_case(seven_ref, sodd_ref))


def forward(fodd, feven, ready, cols, fold):
    edge = jax.ShapeDtypeStruct((cols * 2 * fold // LANES, LANES), F32)
    return pl.pallas_call(
        functools.partial(forward_kernel, fold),
        in_specs=[VMEM] * 3,
        out_specs=[VMEM] * 2,
        out_shape=[edge, edge],
        name="forward",
        compiler_params=PARAMS,
    )(feven, fodd, ready)


def prepare_kernel(layer, w_ref, after_ref, hi_ref, lo_ref, ready_ref, stage, sems):
    copies = [pltpu.make_async_copy(w_ref.at[layer, :, dx], stage.at[dx], sems.at[dx]) for dx in range(3)]
    for copy in copies:
        copy.start()
    for dx, copy in enumerate(copies):
        copy.wait()
        first, mid, last = stage[dx, 0], stage[dx, 1], stage[dx, 2]
        ends = 0.5 * (first + last)
        half = 0.5 * mid
        for m, value in enumerate((first, ends + half, ends - half, last)):
            hi_ref[m, dx], lo_ref[m, dx] = parts(value)
    ready_ref[...] = jnp.zeros_like(ready_ref)


def prepare(weight, layer, after):
    _, _, _, chans, outs = weight.shape
    split = jax.ShapeDtypeStruct((4, 3, chans, outs), BF16)
    return pl.pallas_call(
        functools.partial(prepare_kernel, layer),
        in_specs=[pl.BlockSpec(memory_space=pltpu.HBM), VMEM],
        out_specs=[VMEM] * 3,
        out_shape=[split, split, jax.ShapeDtypeStruct((8, LANES), F32)],
        scratch_shapes=[pltpu.VMEM((3, 3, chans, outs), F32), pltpu.SemaphoreType.DMA((3,))],
        name="prepare",
        compiler_params=pltpu.CompilerParams(vmem_limit_bytes=49 * 2**20),
    )(weight, after)


def inner_kernel(fold, x_ref, feven_ref, fodd_ref, wh_ref, wl_ref, out_ref, partial_ref, beside_ref, shifted, hi, lo):
    rows, cols, chans = x_ref.shape
    pairs = rows // 2

    def write(following, before):
        for r in range(rows):
            shifted[r, :, :LANES] = shifted_lanes(x_ref[r, :, :LANES], following[r], before[r], fold)
            shifted[r, :, LANES:] = x_ref[r, :, LANES:]

    by_parity("frame", lambda: write(feven_ref, fodd_ref), lambda: write(fodd_ref, feven_ref))
    beside_ref[0] = shifted[1]
    beside_ref[1] = shifted[rows - 2]

    def fill(at, value):
        place = slice(at * cols, (at + 1) * cols)
        hi[place], lo[place] = parts(value)

    for p in range(pairs):
        fill(p, shifted[2 * p] + shifted[2 * p + 1])
        fill(pairs + p, shifted[2 * p + 1] - shifted[2 * p])
    for p in range(pairs - 1):
        fill(2 * pairs + p, shifted[2 * p + 1] - shifted[2 * p + 3])
        fill(3 * pairs - 1 + p, shifted[2 * p] - shifted[2 * p + 2])

    def products(m, dx, first, count):
        at = slice(first * cols, (first + count) * cols)
        return dot3(hi[at], lo[at], wh_ref[m, dx], wl_ref[m, dx])

    totals = [None] * rows
    for dx in (1, 0, 2):
        plus = products(1, dx, 0, pairs)
        minus = products(2, dx, pairs, pairs)
        above = products(0, dx, 2 * pairs, pairs - 1)
        below = products(3, dx, 3 * pairs - 1, pairs - 1)
        for p in range(pairs):
            at = slice(p * cols, (p + 1) * cols)
            one = plus[at] + minus[at]
            if p > 0:
                one = one + above[(p - 1) * cols : p * cols]
            two = plus[at] - minus[at]
            if p < pairs - 1:
                two = two - below[p * cols : (p + 1) * cols]
            for r, value in ((2 * p, one), (2 * p + 1, two)):
                value = shift_columns(value, dx)
                totals[r] = value if totals[r] is None else totals[r] + value
    partial_ref[0] = totals[0]
    partial_ref[1] = totals[rows - 1]
    for r in range(1, rows - 1):
        out_ref[r - 1] = jnp.maximum(totals[r], 0.0)


def inner_rows(x, fodd, feven, wh, wl):
    rows, cols, chans = x.shape
    outs = wh.shape[-1]
    products = 4 * (rows // 2) - 2
    return pl.pallas_call(
        functools.partial(inner_kernel, chans // 8),
        in_specs=[VMEM] * 5,
        out_specs=[VMEM] * 3,
        out_shape=[
            jax.ShapeDtypeStruct((rows - 2, cols, outs), F32),
            jax.ShapeDtypeStruct((2, cols, outs), F32),
            jax.ShapeDtypeStruct((2, cols, chans), F32),
        ],
        scratch_shapes=[
            pltpu.VMEM((rows, cols, chans), F32),
            pltpu.VMEM((products * cols, chans), BF16),
            pltpu.VMEM((products * cols, chans), BF16),
        ],
        name="inner_rows",
        compiler_params=PARAMS,
    )(x, feven, fodd, wh, wl)


def outer_kernel(
    fold, final, reven_ref, rodd_ref, sodd_ref, seven_ref, wh_ref, wl_ref, partial_ref, beside_ref, inner_ref, out_ref, *rest
):
    rows, cols, outs = out_ref.shape
    width = 2 * fold
    edges = (0, rows - 1)
    frame_odd = lax.axis_index("frame") % 2 == 1

    def pack_frames(r, row):
        to_before, to_following = pack(row[:, :LANES], 0, fold), pack(row[:, :LANES], fold, fold)
        rest[0][r] = jnp.where(frame_odd, to_before, to_following)
        rest[1][r] = jnp.where(frame_odd, to_following, to_before)

    if final:
        stage, sems = rest
        copies = [pltpu.make_async_copy(stage.at[i], out_ref.at[r], sems.at[i]) for i, r in enumerate(edges)]
        copies.append(pltpu.make_async_copy(inner_ref, out_ref.at[1 : rows - 1], sems.at[2]))
        copies[2].start()
    else:
        out_ref[1 : rows - 1] = inner_ref[...]
        for r in range(1, rows - 1):
            pack_frames(r, inner_ref[r - 1])

    def finish(i, kept_ref, moved_ref):
        halves = LANES // width
        height = cols // halves
        lane = lane_of(height)
        low = []
        for k in range(halves):
            moved = turn(moved_ref[...], -k * width)
            kept = turn(kept_ref[cols:], width - k * width)
            low.append(jnp.where(lane < width, moved, kept))
        halo = jnp.concatenate([jnp.concatenate(low, axis=0), kept_ref[:cols]], axis=1)
        hi, lo = parts(halo - beside_ref[i])
        total = partial_ref[i]
        for dx in range(3):
            total = total + shift_columns(dot3(hi, lo, wh_ref[3 * i, dx], wl_ref[3 * i, dx]), dx)
        total = jnp.maximum(total, 0.0)
        if final:
            stage[i] = total
            copies[i].start()
        else:
            out_ref[edges[i]] = total
            pack_frames(edges[i], total)

    def both(above, below):
        finish(0, *above)
        finish(1, *below)

    odd, even = (rodd_ref, sodd_ref), (reven_ref, seven_ref)
    by_parity("row", lambda: both(odd, even), lambda: both(even, odd))
    if final:
        for copy in copies:
            copy.wait()


def outer_rows(reven, rodd, sodd, seven, wh, wl, partial, beside, inner, final):
    rows, cols, outs = inner.shape
    fold = outs // 8
    field = jax.ShapeDtypeStruct((rows + 2, cols, outs), F32)
    frames = jax.ShapeDtypeStruct((rows + 2, cols * fold // LANES, LANES), F32)
    stage = [pltpu.VMEM((2, cols, outs), F32), pltpu.SemaphoreType.DMA((3,))]
    return pl.pallas_call(
        functools.partial(outer_kernel, fold, final),
        in_specs=[VMEM] * 9,
        out_specs=[pl.BlockSpec(memory_space=pltpu.HBM)] if final else [VMEM] * 3,
        out_shape=[field] if final else [field, frames, frames],
        scratch_shapes=stage if final else [],
        name="outer_rows",
        compiler_params=PARAMS,
    )(reven, rodd, sodd, seven, wh, wl, partial, beside, inner)


def local(features, conv_weight):
    frames, rows, cols, chans = features.shape
    layers = conv_weight.shape[0]
    field = features.reshape(rows, cols, chans)
    to_even, to_odd = frames_to_send(lax.slice_in_dim(field, 0, LANES, axis=2), chans // 8)
    for layer in range(layers):
        feven, fodd = exchange(to_even, "frame", 0), exchange(to_odd, "frame", 1)
        wh, wl, ready = prepare(conv_weight, layer, feven)
        reven, rodd = rows_to_send(field)
        reven, rodd = exchange(reven, "row", 0), exchange(rodd, "row", 1)
        sodd, seven = forward(fodd, feven, ready, cols, chans // 8)
        sodd, seven = exchange(sodd, "row", 1), exchange(seven, "row", 0)
        inner, partial, beside = inner_rows(field, fodd, feven, wh, wl)
        last = layer == layers - 1
        field, *frames_out = outer_rows(reven, rodd, sodd, seven, wh, wl, partial, beside, inner, last)
        if not last:
            to_even, to_odd = frames_out
    return field.reshape(features.shape)


def solution(mesh):
    placed = (P("frame", "row", None, None), P())
    return jax.shard_map(
        local, mesh=mesh, in_specs=placed, out_specs=P("frame", "row", None, None), check_vma=False
    )
```
